32 devices in a mesh: light: 4 (over z), pix: 4 (over x, core), cam: 2 (over y).
Axes of the slice: x: 2, y: 2, z: 4, core: 2. Of those that a mesh axis runs over, the one named last changes fastest.
Arguments:
- reflectance: bfloat16 [1024, 32, 4096], P('light', 'cam', 'pix'), may hold values from -120 to 120
- start_basis: float32 [1024, 128], replicated, may hold values from -6 to 6
Outputs:
- core_tensor: float32 [128, 32, 4096], P('light', 'cam', 'pix')
- light_basis: float32 [1024, 128], P('light')
The draws below stay inside these ranges and needn't reach their ends.
All inputs are finite; a program needn't handle non-finite values.
Results may differ from the reference program's by a relative error of at most 0.015.
Values may be sent and summed in bfloat16 or wider, within the bound.
A program may use at most 128 MiB of HBM per device.

```python
import math
import jax
import jax.numpy as jnp
from jax import lax

L = 1024
C = 32
R = 128
ITERS = 2
P_SIZE = 4096
L_DEV = 256
N_LIGHT = 4


def draw_reflectance(key, part):
    subkeys = jax.random.split(key, 6)
    noise_part = jnp.clip(jax.random.normal(subkeys[0], (L, C, P_SIZE), jnp.float32), -6.0, 6.0)
    pixel_scale = jnp.exp(jax.random.uniform(subkeys[1], (1, 1, P_SIZE), jnp.float32, math.log(0.3), math.log(3.0)))
    strength = 0.035
    light_scale = jnp.exp(jax.random.uniform(subkeys[2], (L, 1, 1), jnp.float32, 0.0, math.log(3.0)))
    camera_scale = jnp.exp(jax.random.uniform(subkeys[3], (1, C, 1), jnp.float32, math.log(0.5), math.log(2.0)))
    loadings = jnp.clip(jax.random.normal(subkeys[4], (4, L), jnp.float32), -4.0, 4.0)
    patterns = jnp.clip(jax.random.normal(subkeys[5], (4, C, P_SIZE), jnp.float32), -4.0, 4.0)
    blended = noise_part
    for factor in range(4):
        blended = blended + strength * loadings[factor][:, None, None] * patterns[factor][None, :, :]
    scaled = blended * light_scale * camera_scale * pixel_scale
    return jnp.clip(scaled, -120.0, 120.0).astype(jnp.bfloat16)


def noise(rng, extent, scale, reach, kind=jnp.bfloat16):
    array = scale * jax.random.normal(rng, extent, jnp.float32)
    return jnp.clip(array, min=-reach, max=reach).astype(kind)


def setup_inputs(seed: int = 0) -> dict:
    arg_keys = jax.random.split(jax.random.key(seed), 3)
    reflectance = draw_reflectance(jax.random.fold_in(arg_keys[2], 71), 0)
    start_basis = noise(arg_keys[1], (L, R), 1.0, 6.0, jnp.float32)
    return dict(reflectance=reflectance, start_basis=start_basis)


def orthonormal(image_full):
    inner_gram = jnp.dot(image_full.T.astype(jnp.float32), image_full.astype(jnp.float32), preferred_element_type=jnp.float32, precision=lax.Precision.HIGHEST)
    factor = jnp.linalg.cholesky(inner_gram)
    return lax.linalg.triangular_solve(factor, image_full, left_side=False, lower=True, transpose_a=True)

def reference(reflectance, start_basis):
    fibers = reflectance.reshape(L, C * P_SIZE).astype(jnp.float32)
    gram = jnp.dot(fibers.astype(jnp.float32), fibers.T.astype(jnp.float32), preferred_element_type=jnp.float32) * (1.0 / (C * P_SIZE))
    basis_now = start_basis
    for iteration in range(ITERS):
        image_full = jnp.dot(gram.astype(jnp.float32), basis_now.astype(jnp.float32), preferred_element_type=jnp.float32, precision=lax.Precision.HIGHEST)
        basis_now = orthonormal(image_full)
    rounded = basis_now.astype(jnp.bfloat16)
    light_blocks = reflectance.reshape(N_LIGHT, L_DEV, C * P_SIZE)
    basis_blocks = rounded.reshape(N_LIGHT, L_DEV, R)

    def add_block(running, paired):
        block_rows, block_basis = paired
        product = jnp.dot(block_basis.astype(jnp.float32).T.astype(jnp.float32), block_rows.astype(jnp.float32), preferred_element_type=jnp.float32)
        narrowed = lax.optimization_barrier(product.astype(jnp.bfloat16))
        return (running + narrowed.astype(jnp.float32), None)
    core_flat, unused = lax.scan(add_block, jnp.zeros((R, C * P_SIZE), jnp.float32), (light_blocks, basis_blocks))
    return (core_flat.reshape(R, C, P_SIZE), basis_now)
```

```python
import functools

import jax
import jax.numpy as jnp
from jax import lax
from jax.experimental import pallas as pl
from jax.experimental.pallas import tpu as pltpu
from jax.sharding import PartitionSpec as P

ITERS = 2
MESH = pl.DeviceIdType.MESH


def greet(barrier, devices):
    for device in devices:
        pl.semaphore_signal(barrier, inc=1, device_id=device, device_id_type=MESH)
    pl.semaphore_wait(barrier, len(devices))


def exchange_kernel(lights, src_ref, dst_ref, bounce, local_sem, send_sem, recv_sem):
    me = lax.axis_index("light")
    peers = [lax.rem(me + step, lights) for step in range(1, lights)]
    greet(pltpu.get_barrier_semaphore(), [{"light": peer} for peer in peers])
    parts, width = src_ref.shape[1], src_ref.shape[3]
    copies = []
    for part in range(parts):
        for slot, peer in enumerate(peers):
            copy = pltpu.make_async_remote_copy(
                src_ref=src_ref.at[peer, part],
                dst_ref=dst_ref.at[me, :, pl.ds(part * width, width)],
                send_sem=send_sem.at[slot, part],
                recv_sem=recv_sem.at[slot, part],
                device_id={"light": peer},
                device_id_type=MESH,
            )
            copy.start()
            copies.append(copy)
    for part in range(parts):
        inward = pltpu.make_async_copy(src_ref.at[me, part], bounce.at[part], local_sem.at[0, part])
        inward.start()
        inward.wait()
        outward = pltpu.make_async_copy(
            bounce.at[part], dst_ref.at[me, :, pl.ds(part * width, width)], local_sem.at[1, part]
        )
        outward.start()
        outward.wait()
    for copy in copies:
        copy.wait()


def exchange(blocks, collective_id):
    lights, parts, rows, width = blocks.shape
    return pl.pallas_call(
        functools.partial(exchange_kernel, lights),
        out_shape=jax.ShapeDtypeStruct((lights, rows, parts * width), blocks.dtype),
        in_specs=[pl.BlockSpec(memory_space=pl.ANY)],
        out_specs=pl.BlockSpec(memory_space=pl.ANY),
        scratch_shapes=[
            pltpu.VMEM(blocks.shape[1:], blocks.dtype),
            pltpu.SemaphoreType.DMA((2, parts)),
            pltpu.SemaphoreType.DMA((lights - 1, parts)),
            pltpu.SemaphoreType.DMA((lights - 1, parts)),
        ],
        compiler_params=pltpu.CompilerParams(
            collective_id=collective_id, has_side_effects=True
        ),
    )(blocks)


def total_kernel(lights, pixes, cams, part_ref, out_ref, plane_buf, light_buf, own_buf,
                 send1, recv1, send2, recv2, send3, recv3):
    light = lax.axis_index("light")
    plane = pixes * cams
    me = lax.axis_index("pix") * cams + lax.axis_index("cam")
    rows = part_ref.shape[0] // plane

    def row_slice(index):
        return pl.ds(pl.multiple_of(index * rows, rows), rows)

    peers = [lax.rem(me + step, plane) for step in range(1, plane)]
    plane_devices = [{"pix": peer // cams, "cam": lax.rem(peer, cams)} for peer in peers]
    light_devices = [{"light": lax.rem(light + step, lights)} for step in range(1, lights)]
    greet(pltpu.get_barrier_semaphore(), plane_devices + light_devices)

    copies = []
    for slot, (peer, device) in enumerate(zip(peers, plane_devices)):
        copy = pltpu.make_async_remote_copy(
            src_ref=part_ref.at[row_slice(peer)],
            dst_ref=plane_buf.at[slot],
            send_sem=send1.at[slot],
            recv_sem=recv1.at[slot],
            device_id=device,
            device_id_type=MESH,
        )
        copy.start()
        copies.append(copy)
    total = part_ref[row_slice(me), :].astype(jnp.float32)
    for slot, copy in enumerate(copies):
        copy.wait_recv()
        total += plane_buf[slot].astype(jnp.float32)
    own_buf[...] = total.astype(own_buf.dtype)

    light_copies = []
    for slot, device in enumerate(light_devices):
        copy = pltpu.make_async_remote_copy(
            src_ref=own_buf,
            dst_ref=light_buf.at[light],
            send_sem=send2.at[slot],
            recv_sem=recv2.at[slot],
            device_id=device,
            device_id_type=MESH,
        )
        copy.start()
        light_copies.append(copy)
    light_buf[light] = own_buf[...]
    for copy in light_copies:
        copy.wait_recv()
    total = light_buf[0].astype(jnp.float32)
    for index in range(1, lights):
        total += light_buf[index].astype(jnp.float32)
    out_ref[row_slice(me), :] = total.astype(out_ref.dtype)

    last_copies = []
    for slot, device in enumerate(plane_devices):
        copy = pltpu.make_async_remote_copy(
            src_ref=out_ref.at[row_slice(me)],
            dst_ref=out_ref.at[row_slice(me)],
            send_sem=send3.at[slot],
            recv_sem=recv3.at[slot],
            device_id=device,
            device_id_type=MESH,
        )
        copy.start()
        last_copies.append(copy)
    for copy in copies + light_copies:
        copy.wait_send()
    for copy in last_copies:
        copy.wait()


def total_over_all(part, collective_id):
    lights, pixes, cams = (lax.axis_size(name) for name in ("light", "pix", "cam"))
    plane = pixes * cams
    rows = part.shape[0] // plane
    block = (rows, part.shape[1])
    dma = pltpu.SemaphoreType.DMA
    return pl.pallas_call(
        functools.partial(total_kernel, lights, pixes, cams),
        out_shape=jax.ShapeDtypeStruct(part.shape, part.dtype),
        in_specs=[pl.BlockSpec(memory_space=pltpu.VMEM)],
        out_specs=pl.BlockSpec(memory_space=pltpu.VMEM),
        scratch_shapes=[
            pltpu.VMEM((plane - 1,) + block, part.dtype),
            pltpu.VMEM((lights,) + block, part.dtype),
            pltpu.VMEM(block, part.dtype),
            dma((plane - 1,)), dma((plane - 1,)),
            dma((lights - 1,)), dma((lights - 1,)),
            dma((plane - 1,)), dma((plane - 1,)),
        ],
        compiler_params=pltpu.CompilerParams(
            collective_id=collective_id, has_side_effects=True
        ),
    )(part)


def orthonormal(image_full):
    inner_gram = jnp.dot(
        image_full.T,
        image_full,
        preferred_element_type=jnp.float32,
        precision=lax.Precision.HIGHEST,
    )
    factor = jnp.linalg.cholesky(inner_gram)
    return lax.linalg.triangular_solve(
        factor, image_full, left_side=False, lower=True, transpose_a=True
    )


def per_device(reflectance, start_basis):
    light_rows, camera_cols, pixels = reflectance.shape
    rank_total = start_basis.shape[1]
    light_count = lax.axis_size("light")
    position = lax.axis_index("light")
    inverse_cols = 1.0 / (camera_cols * pixels * lax.axis_size("cam") * lax.axis_size("pix"))
    own_cols = camera_cols // light_count * pixels
    blocks = reflectance.transpose(1, 0, 2).reshape(light_count, -1, light_rows, pixels)
    every_light = exchange(blocks, 0).reshape(light_rows * light_count, own_cols)

    basis_now = start_basis
    for iteration in range(ITERS):
        high = lax.reduce_precision(basis_now, 8, 7)
        pair = jnp.concatenate([high, basis_now - high], axis=1).astype(jnp.bfloat16)
        halves = lax.dot_general(
            pair, every_light, (((0,), (0,)), ((), ())), preferred_element_type=jnp.float32
        )
        projected = (halves[:rank_total] + halves[rank_total:]).astype(jnp.bfloat16)
        image_part = lax.dot_general(
            every_light, projected, (((1,), (1,)), ((), ())), preferred_element_type=jnp.float32
        )
        image_full = total_over_all((image_part * inverse_cols).astype(jnp.bfloat16), 1)
        basis_now = orthonormal(image_full.astype(jnp.float32))
    basis_rows = lax.dynamic_slice_in_dim(basis_now, position * light_rows, light_rows, 0)
    rank_rows = rank_total // light_count
    core = lax.dot_general(
        basis_now.astype(jnp.bfloat16), every_light, (((0,), (0,)), ((), ())),
        preferred_element_type=jnp.float32,
    ).astype(jnp.bfloat16)
    core_rows = exchange(core.reshape(light_count, 1, rank_rows, own_cols), 2)
    core_rows = core_rows.transpose(1, 0, 2).astype(jnp.float32)
    return (core_rows.reshape(rank_rows, camera_cols, pixels), basis_rows)


def solution(mesh):
    placed = (P("light", "cam", "pix"), P())
    return jax.shard_map(
        per_device,
        mesh=mesh,
        in_specs=placed,
        out_specs=(P("light", "cam", "pix"), P("light", None)),
        check_vma=False,
    )
```

```python
import functools

import jax
import jax.numpy as jnp
from jax import lax
from jax.experimental import pallas as pl
from jax.experimental.pallas import tpu as pltpu
from jax.sharding import PartitionSpec as P

ITERS = 2
MESH = pl.DeviceIdType.MESH


def greet(barrier, devices):
    for device in devices:
        pl.semaphore_signal(barrier, inc=1, device_id=device, device_id_type=MESH)
    pl.semaphore_wait(barrier, len(devices))


def exchange_kernel(lights, src_ref, dst_ref, bounce, local_sem, send_sem, recv_sem):
    me = lax.axis_index("light")
    peers = [lax.rem(me + step, lights) for step in range(1, lights)]
    greet(pltpu.get_barrier_semaphore(), [{"light": peer} for peer in peers])
    parts, width = src_ref.shape[1], src_ref.shape[3]
    copies = []
    for part in range(parts):
        for slot, peer in enumerate(peers):
            copy = pltpu.make_async_remote_copy(
                src_ref=src_ref.at[peer, part],
                dst_ref=dst_ref.at[me, :, pl.ds(part * width, width)],
                send_sem=send_sem.at[slot, part],
                recv_sem=recv_sem.at[slot, part],
                device_id={"light": peer},
                device_id_type=MESH,
            )
            copy.start()
            copies.append(copy)
    for part in range(parts):
        inward = pltpu.make_async_copy(src_ref.at[me, part], bounce.at[part], local_sem.at[0, part])
        inward.start()
        inward.wait()
        outward = pltpu.make_async_copy(
            bounce.at[part], dst_ref.at[me, :, pl.ds(part * width, width)], local_sem.at[1, part]
        )
        outward.start()
        outward.wait()
    for copy in copies:
        copy.wait()


def exchange(blocks, collective_id):
    lights, parts, rows, width = blocks.shape
    return pl.pallas_call(
        functools.partial(exchange_kernel, lights),
        out_shape=jax.ShapeDtypeStruct((lights, rows, parts * width), blocks.dtype),
        in_specs=[pl.BlockSpec(memory_space=pl.ANY)],
        out_specs=pl.BlockSpec(memory_space=pl.ANY),
        scratch_shapes=[
            pltpu.VMEM(blocks.shape[1:], blocks.dtype),
            pltpu.SemaphoreType.DMA((2, parts)),
            pltpu.SemaphoreType.DMA((lights - 1, parts)),
            pltpu.SemaphoreType.DMA((lights - 1, parts)),
        ],
        compiler_params=pltpu.CompilerParams(
            collective_id=collective_id, has_side_effects=True
        ),
    )(blocks)


def total_kernel(lights, pixes, cams, part_ref, out_ref, plane_buf, light_buf, own_buf,
                 send1, recv1, send2, recv2, send3, recv3):
    light = lax.axis_index("light")
    plane = pixes * cams
    me = lax.axis_index("pix") * cams + lax.axis_index("cam")
    rows = part_ref.shape[0] // plane

    def row_slice(index):
        return pl.ds(pl.multiple_of(index * rows, rows), rows)

    peers = [lax.rem(me + step, plane) for step in range(1, plane)]
    plane_devices = [{"pix": peer // cams, "cam": lax.rem(peer, cams)} for peer in peers]
    light_devices = [{"light": lax.rem(light + step, lights)} for step in range(1, lights)]
    greet(pltpu.get_barrier_semaphore(), plane_devices + light_devices)

    copies = []
    for slot, (peer, device) in enumerate(zip(peers, plane_devices)):
        copy = pltpu.make_async_remote_copy(
            src_ref=part_ref.at[row_slice(peer)],
            dst_ref=plane_buf.at[slot],
            send_sem=send1.at[slot],
            recv_sem=recv1.at[slot],
            device_id=device,
            device_id_type=MESH,
        )
        copy.start()
        copies.append(copy)
    total = part_ref[row_slice(me), :].astype(jnp.float32)
    for slot, copy in enumerate(copies):
        copy.wait_recv()
        total += plane_buf[slot].astype(jnp.float32)
    own_buf[...] = total.astype(own_buf.dtype)

    light_copies = []
    for slot, device in enumerate(light_devices):
        copy = pltpu.make_async_remote_copy(
            src_ref=own_buf,
            dst_ref=light_buf.at[light],
            send_sem=send2.at[slot],
            recv_sem=recv2.at[slot],
            device_id=device,
            device_id_type=MESH,
        )
        copy.start()
        light_copies.append(copy)
    light_buf[light] = own_buf[...]
    for copy in light_copies:
        copy.wait_recv()
    total = light_buf[0].astype(jnp.float32)
    for index in range(1, lights):
        total += light_buf[index].astype(jnp.float32)
    out_ref[row_slice(me), :] = total.astype(out_ref.dtype)

    last_copies = []
    for slot, device in enumerate(plane_devices):
        copy = pltpu.make_async_remote_copy(
            src_ref=out_ref.at[row_slice(me)],
            dst_ref=out_ref.at[row_slice(me)],
            send_sem=send3.at[slot],
            recv_sem=recv3.at[slot],
            device_id=device,
            device_id_type=MESH,
        )
        copy.start()
        last_copies.append(copy)
    for copy in copies + light_copies:
        copy.wait_send()
    for copy in last_copies:
        copy.wait()


def total_over_all(part, collective_id):
    lights, pixes, cams = (lax.axis_size(name) for name in ("light", "pix", "cam"))
    plane = pixes * cams
    rows = part.shape[0] // plane
    block = (rows, part.shape[1])
    dma = pltpu.SemaphoreType.DMA
    return pl.pallas_call(
        functools.partial(total_kernel, lights, pixes, cams),
        out_shape=jax.ShapeDtypeStruct(part.shape, part.dtype),
        in_specs=[pl.BlockSpec(memory_space=pltpu.VMEM)],
        out_specs=pl.BlockSpec(memory_space=pltpu.VMEM),
        scratch_shapes=[
            pltpu.VMEM((plane - 1,) + block, part.dtype),
            pltpu.VMEM((lights,) + block, part.dtype),
            pltpu.VMEM(block, part.dtype),
            dma((plane - 1,)), dma((plane - 1,)),
            dma((lights - 1,)), dma((lights - 1,)),
            dma((plane - 1,)), dma((plane - 1,)),
        ],
        compiler_params=pltpu.CompilerParams(
            collective_id=collective_id, has_side_effects=True
        ),
    )(part)


def orthonormal_kernel(image_ref, basis_ref, pair_ref):
    image = image_ref[...]
    rank = image.shape[1]
    inner = lax.dot_general(image, image, (((0,), (0,)), ((), ())), preferred_element_type=jnp.float32)
    height = 8
    shape = (height, rank)
    sub = lax.broadcasted_iota(jnp.int32, shape, 0)
    lane = lax.broadcasted_iota(jnp.int32, shape, 1)
    count = rank // height
    left = [inner[height * t : height * (t + 1), :] for t in range(count)]
    right = [jnp.where(lane == sub + height * t, 1.0, 0.0) for t in range(count)]

    def spread_row(tile, k):
        return jnp.broadcast_to(tile[k : k + 1, :], shape)

    def spread_column(tile, j):
        return jnp.broadcast_to(tile[:, j : j + 1], shape)

    for p in range(count):
        first = height * p
        top, below = left[p], right[p]
        columns = [spread_column(top, first + k) for k in range(height)]
        inverses, pivots = [], jnp.ones(shape, jnp.float32)
        for k in range(height):
            pivot = spread_row(columns[k], k)
            inverse = 1.0 / pivot
            pivots = jnp.where(sub == k, pivot, pivots)
            inverses.append(inverse)
            factor = jnp.where(sub > k, columns[k] * inverse, 0.0)
            for later in range(k + 1, height):
                columns[later] = columns[later] - factor * spread_row(columns[later], k)
            top = top - factor * spread_row(top, k)
            below = below - factor * spread_row(below, k)
        right[p] = below * lax.rsqrt(pivots)
        top_rows = [spread_row(top, k) * inverses[k] for k in range(height)]
        below_rows = [spread_row(below, k) * inverses[k] for k in range(height)]
        steps = [
            [spread_row(columns[later], k) * inverses[k] for later in range(k + 1, height)]
            for k in range(height)
        ]
        for t in range(p + 1, count):
            own = [spread_column(left[t], first + k) for k in range(height)]
            upper, lower = left[t], right[t]
            for k in range(height):
                for index, later in enumerate(range(k + 1, height)):
                    own[later] = own[later] - own[k] * steps[k][index]
                upper = upper - own[k] * top_rows[k]
                lower = lower - own[k] * below_rows[k]
            left[t], right[t] = upper, lower
    inverse = jnp.concatenate(right, axis=0)
    pieces = []
    for _ in range(3):
        piece = inverse.astype(jnp.bfloat16)
        pieces.append(piece)
        inverse = inverse - piece.astype(jnp.float32)
    basis = None
    for piece in reversed(pieces):
        term = lax.dot_general(
            image, piece, (((1,), (1,)), ((), ())), preferred_element_type=jnp.float32
        )
        basis = term if basis is None else basis + term
    basis_ref[...] = basis
    high = basis.astype(jnp.bfloat16)
    pair_ref[:, :rank] = high
    pair_ref[:, rank:] = (basis - high.astype(jnp.float32)).astype(jnp.bfloat16)


def orthonormal(image):
    rows, rank = image.shape
    vmem = pl.BlockSpec(memory_space=pltpu.VMEM)
    return pl.pallas_call(
        orthonormal_kernel,
        out_shape=(
            jax.ShapeDtypeStruct((rows, rank), jnp.float32),
            jax.ShapeDtypeStruct((rows, 2 * rank), jnp.bfloat16),
        ),
        in_specs=[vmem],
        out_specs=(vmem, vmem),
    )(image)


def per_device(reflectance, start_basis):
    light_rows, camera_cols, pixels = reflectance.shape
    rank_total = start_basis.shape[1]
    light_count = lax.axis_size("light")
    position = lax.axis_index("light")
    inverse_cols = 1.0 / (camera_cols * pixels * lax.axis_size("cam") * lax.axis_size("pix"))
    own_cols = camera_cols // light_count * pixels
    blocks = reflectance.transpose(1, 0, 2).reshape(light_count, -1, light_rows, pixels)
    every_light = exchange(blocks, 0).reshape(light_rows * light_count, own_cols)

    high = lax.reduce_precision(start_basis, 8, 7)
    pair = jnp.concatenate([high, start_basis - high], axis=1).astype(jnp.bfloat16)
    for iteration in range(ITERS):
        halves = lax.dot_general(
            pair, every_light, (((0,), (0,)), ((), ())), preferred_element_type=jnp.float32
        )
        projected = (halves[:rank_total] + halves[rank_total:]).astype(jnp.bfloat16)
        image_part = lax.dot_general(
            every_light, projected, (((1,), (1,)), ((), ())), preferred_element_type=jnp.float32
        )
        image_full = total_over_all((image_part * inverse_cols).astype(jnp.bfloat16), 1)
        basis_now, pair = orthonormal(image_full)
    basis_rows = lax.dynamic_slice_in_dim(basis_now, position * light_rows, light_rows, 0)
    rank_rows = rank_total // light_count
    core = lax.dot_general(
        pair[:, :rank_total], every_light, (((0,), (0,)), ((), ())),
        preferred_element_type=jnp.float32,
    ).astype(jnp.bfloat16)
    core_rows = exchange(core.reshape(light_count, 1, rank_rows, own_cols), 2)
    core_rows = core_rows.transpose(1, 0, 2).astype(jnp.float32)
    return (core_rows.reshape(rank_rows, camera_cols, pixels), basis_rows)


def solution(mesh):
    placed = (P("light", "cam", "pix"), P())
    return jax.shard_map(
        per_device,
        mesh=mesh,
        in_specs=placed,
        out_specs=(P("light", "cam", "pix"), P("light", None)),
        check_vma=False,
    )
```

```python
import functools

import jax
import jax.numpy as jnp
from jax import lax
from jax.experimental import pallas as pl
from jax.experimental.pallas import tpu as pltpu
from jax.sharding import PartitionSpec as P

ITERS = 2
MESH = pl.DeviceIdType.MESH


def greet(barrier, devices):
    for device in devices:
        pl.semaphore_signal(barrier, inc=1, device_id=device, device_id_type=MESH)
    pl.semaphore_wait(barrier, len(devices))


def exchange_kernel(lights, src_ref, dst_ref, bounce, local_sem, send_sem, recv_sem):
    me = lax.axis_index("light")
    barrier = pltpu.get_barrier_semaphore()
    greet(barrier, [{"light": lax.rem(me + step, lights)} for step in range(1, lights)])
    parts, width = src_ref.shape[1], src_ref.shape[3]

    def both_ways(action):
        for distance in range(1, lights):
            for side in range(2):
                peer = me + distance if side == 0 else me - distance
                inside = peer < lights if side == 0 else peer >= 0
                pl.when(inside)(functools.partial(action, peer, 2 * (distance - 1) + side))

    def copy_of(peer, slot, part):
        return pltpu.make_async_remote_copy(
            src_ref=src_ref.at[peer, part],
            dst_ref=dst_ref.at[me, :, pl.ds(part * width, width)],
            send_sem=send_sem.at[slot, part],
            recv_sem=recv_sem.at[slot, part],
            device_id={"light": peer},
            device_id_type=MESH,
        )

    def start(peer, slot):
        for part in range(parts):
            copy_of(peer, slot, part).start()

    def finish(peer, slot):
        opposite = slot + 1 - 2 * (slot % 2)
        for part in range(parts):
            copy_of(peer, slot, part).wait_send()
            copy_of(peer, opposite, part).wait_recv()

    both_ways(start)
    for part in range(parts):
        inward = pltpu.make_async_copy(src_ref.at[me, part], bounce.at[part], local_sem.at[0, part])
        inward.start()
        inward.wait()
        outward = pltpu.make_async_copy(
            bounce.at[part], dst_ref.at[me, :, pl.ds(part * width, width)], local_sem.at[1, part]
        )
        outward.start()
        outward.wait()
    both_ways(finish)


def exchange(blocks, collective_id):
    lights, parts, rows, width = blocks.shape
    return pl.pallas_call(
        functools.partial(exchange_kernel, lights),
        out_shape=jax.ShapeDtypeStruct((lights, rows, parts * width), blocks.dtype),
        in_specs=[pl.BlockSpec(memory_space=pl.ANY)],
        out_specs=pl.BlockSpec(memory_space=pl.ANY),
        scratch_shapes=[
            pltpu.VMEM(blocks.shape[1:], blocks.dtype),
            pltpu.SemaphoreType.DMA((2, parts)),
            pltpu.SemaphoreType.DMA((2 * (lights - 1), parts)),
            pltpu.SemaphoreType.DMA((2 * (lights - 1), parts)),
        ],
        compiler_params=pltpu.CompilerParams(
            collective_id=collective_id, has_side_effects=True
        ),
    )(blocks)


def total_kernel(lights, pixes, cams, part_ref, out_ref, plane_buf, light_buf, own_buf,
                 send1, recv1, send2, recv2, send3, recv3):
    light = lax.axis_index("light")
    plane = pixes * cams
    me = lax.axis_index("pix") * cams + lax.axis_index("cam")
    rows = part_ref.shape[0] // plane

    def row_slice(index):
        return pl.ds(pl.multiple_of(index * rows, rows), rows)

    peers = [lax.rem(me + step, plane) for step in range(1, plane)]
    plane_devices = [{"pix": peer // cams, "cam": lax.rem(peer, cams)} for peer in peers]
    light_devices = [{"light": lax.rem(light + step, lights)} for step in range(1, lights)]
    greet(pltpu.get_barrier_semaphore(), plane_devices + light_devices)

    copies = []
    for slot, (peer, device) in enumerate(zip(peers, plane_devices)):
        copy = pltpu.make_async_remote_copy(
            src_ref=part_ref.at[row_slice(peer)],
            dst_ref=plane_buf.at[slot],
            send_sem=send1.at[slot],
            recv_sem=recv1.at[slot],
            device_id=device,
            device_id_type=MESH,
        )
        copy.start()
        copies.append(copy)
    total = part_ref[row_slice(me), :].astype(jnp.float32)
    for slot, copy in enumerate(copies):
        copy.wait_recv()
        total += plane_buf[slot].astype(jnp.float32)
    own_buf[...] = total.astype(own_buf.dtype)

    light_copies = []
    for slot, device in enumerate(light_devices):
        copy = pltpu.make_async_remote_copy(
            src_ref=own_buf,
            dst_ref=light_buf.at[light],
            send_sem=send2.at[slot],
            recv_sem=recv2.at[slot],
            device_id=device,
            device_id_type=MESH,
        )
        copy.start()
        light_copies.append(copy)
    light_buf[light] = own_buf[...]
    for copy in light_copies:
        copy.wait_recv()
    total = light_buf[0].astype(jnp.float32)
    for index in range(1, lights):
        total += light_buf[index].astype(jnp.float32)
    out_ref[row_slice(me), :] = total.astype(out_ref.dtype)

    last_copies = []
    for slot, device in enumerate(plane_devices):
        copy = pltpu.make_async_remote_copy(
            src_ref=out_ref.at[row_slice(me)],
            dst_ref=out_ref.at[row_slice(me)],
            send_sem=send3.at[slot],
            recv_sem=recv3.at[slot],
            device_id=device,
            device_id_type=MESH,
        )
        copy.start()
        last_copies.append(copy)
    for copy in copies + light_copies:
        copy.wait_send()
    for copy in last_copies:
        copy.wait()


def total_over_all(part, collective_id):
    lights, pixes, cams = (lax.axis_size(name) for name in ("light", "pix", "cam"))
    plane = pixes * cams
    rows = part.shape[0] // plane
    block = (rows, part.shape[1])
    dma = pltpu.SemaphoreType.DMA
    return pl.pallas_call(
        functools.partial(total_kernel, lights, pixes, cams),
        out_shape=jax.ShapeDtypeStruct(part.shape, part.dtype),
        in_specs=[pl.BlockSpec(memory_space=pltpu.VMEM)],
        out_specs=pl.BlockSpec(memory_space=pltpu.VMEM),
        scratch_shapes=[
            pltpu.VMEM((plane - 1,) + block, part.dtype),
            pltpu.VMEM((lights,) + block, part.dtype),
            pltpu.VMEM(block, part.dtype),
            dma((plane - 1,)), dma((plane - 1,)),
            dma((lights - 1,)), dma((lights - 1,)),
            dma((plane - 1,)), dma((plane - 1,)),
        ],
        compiler_params=pltpu.CompilerParams(
            collective_id=collective_id, has_side_effects=True
        ),
    )(part)


def orthonormal_kernel(image_ref, basis_ref, pair_ref, whole):
    image = image_ref[...]
    rank = image.shape[1]
    inner = lax.dot_general(image, image, (((0,), (0,)), ((), ())), preferred_element_type=jnp.float32)
    height = 8
    shape = (height, rank)
    sub = lax.broadcasted_iota(jnp.int32, shape, 0)
    lane = lax.broadcasted_iota(jnp.int32, shape, 1)
    count = rank // height
    left = [inner[height * t : height * (t + 1), :] for t in range(count)]
    right = [jnp.where(lane == sub + height * t, 1.0, 0.0) for t in range(count)]

    def spread_row(tile, k):
        return jnp.broadcast_to(tile[k : k + 1, :], shape)

    def spread_column(tile, j):
        return jnp.broadcast_to(tile[:, j : j + 1], shape)

    for p in range(count):
        first = height * p
        top, below = left[p], right[p]
        columns = [spread_column(top, first + k) for k in range(height)]
        inverses, pivots = [], jnp.ones(shape, jnp.float32)
        for k in range(height):
            pivot = spread_row(columns[k], k)
            inverse = 1.0 / pivot
            pivots = jnp.where(sub == k, pivot, pivots)
            inverses.append(inverse)
            factor = jnp.where(sub > k, columns[k] * inverse, 0.0)
            for later in range(k + 1, height):
                columns[later] = columns[later] - factor * spread_row(columns[later], k)
            top = top - factor * spread_row(top, k)
            below = below - factor * spread_row(below, k)
        right[p] = below * lax.rsqrt(pivots)
        top_rows = [spread_row(top, k) * inverses[k] for k in range(height)]
        below_rows = [spread_row(below, k) * inverses[k] for k in range(height)]
        steps = [
            [spread_row(columns[later], k) * inverses[k] for later in range(k + 1, height)]
            for k in range(height)
        ]
        for t in range(p + 1, count):
            own = [spread_column(left[t], first + k) for k in range(height)]
            upper, lower = left[t], right[t]
            for k in range(height):
                for index, later in enumerate(range(k + 1, height)):
                    own[later] = own[later] - own[k] * steps[k][index]
                upper = upper - own[k] * top_rows[k]
                lower = lower - own[k] * below_rows[k]
            left[t], right[t] = upper, lower
    inverse = jnp.concatenate(right, axis=0)
    pieces = []
    for _ in range(3):
        piece = inverse.astype(jnp.bfloat16)
        pieces.append(piece)
        inverse = inverse - piece.astype(jnp.float32)
    basis = None
    for piece in reversed(pieces):
        term = lax.dot_general(
            image, piece, (((1,), (1,)), ((), ())), preferred_element_type=jnp.float32
        )
        basis = term if basis is None else basis + term
    whole[...] = basis
    own = basis_ref.shape[0]
    basis_ref[...] = whole[pl.ds(pl.multiple_of(lax.axis_index("light") * own, own), own), :]
    high = basis.astype(jnp.bfloat16)
    pair_ref[:, :rank] = high
    pair_ref[:, rank:] = (basis - high.astype(jnp.float32)).astype(jnp.bfloat16)


def orthonormal(image):
    rows, rank = image.shape
    own = rows // lax.axis_size("light")
    vmem = pl.BlockSpec(memory_space=pltpu.VMEM)
    return pl.pallas_call(
        orthonormal_kernel,
        out_shape=(
            jax.ShapeDtypeStruct((own, rank), jnp.float32),
            jax.ShapeDtypeStruct((rows, 2 * rank), jnp.bfloat16),
        ),
        in_specs=[vmem],
        out_specs=(vmem, vmem),
        scratch_shapes=[pltpu.VMEM((rows, rank), jnp.float32)],
    )(image)


def per_device(reflectance, start_basis):
    light_rows, camera_cols, pixels = reflectance.shape
    rank_total = start_basis.shape[1]
    light_count = lax.axis_size("light")
    inverse_cols = 1.0 / (camera_cols * pixels * lax.axis_size("cam") * lax.axis_size("pix"))
    own_cols = camera_cols // light_count * pixels
    blocks = reflectance.transpose(1, 0, 2).reshape(light_count, -1, light_rows, pixels)
    every_light = exchange(blocks, 0).reshape(light_rows * light_count, own_cols)

    high = lax.reduce_precision(start_basis, 8, 7)
    pair = jnp.concatenate([high, start_basis - high], axis=1).astype(jnp.bfloat16)
    for iteration in range(ITERS):
        halves = lax.dot_general(
            pair, every_light, (((0,), (0,)), ((), ())), preferred_element_type=jnp.float32
        )
        projected = (halves[:rank_total] + halves[rank_total:]).astype(jnp.bfloat16)
        image_part = lax.dot_general(
            every_light, projected, (((1,), (1,)), ((), ())), preferred_element_type=jnp.float32
        )
        image_full = total_over_all((image_part * inverse_cols).astype(jnp.bfloat16), 1)
        basis_rows, pair = orthonormal(image_full)
    rank_rows = rank_total // light_count
    core = lax.dot_general(
        pair[:, :rank_total], every_light, (((0,), (0,)), ((), ())),
        preferred_element_type=jnp.float32,
    ).astype(jnp.bfloat16)
    core_rows = exchange(core.reshape(light_count, 1, rank_rows, own_cols), 2)
    core_rows = core_rows.transpose(1, 0, 2).astype(jnp.float32)
    return (core_rows.reshape(rank_rows, camera_cols, pixels), basis_rows)


def solution(mesh):
    placed = (P("light", "cam", "pix"), P())
    return jax.shard_map(
        per_device,
        mesh=mesh,
        in_specs=placed,
        out_specs=(P("light", "cam", "pix"), P("light", None)),
        check_vma=False,
    )
```

```python
import functools

import jax
import jax.numpy as jnp
from jax import lax
from jax.experimental import pallas as pl
from jax.experimental.pallas import tpu as pltpu
from jax.sharding import PartitionSpec as P

ITERS = 2
MESH = pl.DeviceIdType.MESH


def greet(barrier, devices):
    for device in devices:
        pl.semaphore_signal(barrier, inc=1, device_id=device, device_id_type=MESH)
    pl.semaphore_wait(barrier, len(devices))


def gather_kernel(lights, blocks, scale, source_ref, pair_ref, every_ref, image_ref, arrived, turned, tile, left, total,
                  load_sem, own_sem, tile_sem, send_sem, recv_sem, first_send, first_recv):
    me = lax.axis_index("light")
    rows, cams, width = source_ref.shape
    parts = cams // lights
    rank = image_ref.shape[1]
    height = rows // blocks
    step_rows = 16
    peers = [lax.rem(me + step, lights) for step in range(1, lights)]

    def load(block):
        return pltpu.make_async_copy(
            source_ref.at[pl.ds(block * height, height)], arrived.at[block % 2], load_sem.at[block % 2]
        )

    load(0).start()
    greet(pltpu.get_barrier_semaphore(), [{"light": peer} for peer in peers])

    def columns(part):
        return pl.ds(part * width, width)

    def first_copy(slot, peer, block):
        span = pl.ds(block * height, height)
        return pltpu.make_async_remote_copy(
            src_ref=turned.at[peer * parts, span],
            dst_ref=every_ref.at[me, span, columns(0)],
            send_sem=first_send.at[slot, block],
            recv_sem=first_recv.at[slot, block],
            device_id={"light": peer},
            device_id_type=MESH,
        )

    def later_copy(slot, peer, part):
        return pltpu.make_async_remote_copy(
            src_ref=turned.at[peer * parts + part],
            dst_ref=every_ref.at[me, :, columns(part)],
            send_sem=send_sem.at[slot, part],
            recv_sem=recv_sem.at[slot, part],
            device_id={"light": peer},
            device_id_type=MESH,
        )

    copies = [[] for _ in range(parts)]
    for block in range(blocks):
        if block + 1 < blocks:
            load(block + 1).start()
        load(block).wait()

        def turn(index, carry):
            start = pl.multiple_of(index * step_rows, step_rows)
            turned[:, pl.ds(pl.multiple_of(block * height + start, step_rows), step_rows), :] = jnp.transpose(
                arrived[block % 2, pl.ds(start, step_rows)], (1, 0, 2)
            )
            return carry

        lax.fori_loop(0, height // step_rows, turn, 0)
        for slot, peer in enumerate(peers):
            copies[0].append(first_copy(slot, peer, block))
            copies[0][-1].start()
    for part in range(1, parts):
        for slot, peer in enumerate(peers):
            copies[part].append(later_copy(slot, peer, part))
            copies[part][-1].start()
    own = [
        pltpu.make_async_copy(turned.at[me * parts + part], every_ref.at[me, :, columns(part)], own_sem.at[part])
        for part in range(parts)
    ]
    for copy in own:
        copy.start()

    left[...] = pair_ref[...].T
    total[...] = jnp.zeros_like(total)
    chunk = 256
    for part in range(parts):
        own[part].wait()
        for copy in copies[part]:
            copy.wait_recv()
        reads = [
            pltpu.make_async_copy(
                every_ref.at[light, :, columns(part)], tile.at[pl.ds(light * rows, rows)], tile_sem.at[light]
            )
            for light in range(lights)
        ]
        for read in reads:
            read.start()
        for read in reads:
            read.wait()

        def products(index, carry):
            some = tile[:, pl.ds(pl.multiple_of(index * chunk, chunk), chunk)]
            halves = jnp.dot(left[...], some, preferred_element_type=jnp.float32)
            projected = (halves[:rank] + halves[rank:]).astype(jnp.bfloat16)
            total[...] += lax.dot_general(
                some, projected, (((1,), (1,)), ((), ())), preferred_element_type=jnp.float32
            )
            return carry

        lax.fori_loop(0, width // chunk, products, 0)
    image_ref[...] = (total[...] * scale).astype(image_ref.dtype)
    for group in copies:
        for copy in group:
            copy.wait_send()


def gather_lights(reflectance, pair, scale, collective_id):
    rows, cams, width = reflectance.shape
    lights = lax.axis_size("light")
    parts = cams // lights
    blocks = max(1, rows // 64)
    rank = pair.shape[1] // 2
    vmem, anywhere = pl.BlockSpec(memory_space=pltpu.VMEM), pl.BlockSpec(memory_space=pl.ANY)
    dma = pltpu.SemaphoreType.DMA
    return pl.pallas_call(
        functools.partial(gather_kernel, lights, blocks, scale),
        out_shape=(
            jax.ShapeDtypeStruct((lights, rows, parts * width), reflectance.dtype),
            jax.ShapeDtypeStruct((lights * rows, rank), jnp.bfloat16),
        ),
        in_specs=[anywhere, vmem],
        out_specs=(anywhere, vmem),
        scratch_shapes=[
            pltpu.VMEM((2, rows // blocks, cams, width), reflectance.dtype),
            pltpu.VMEM((cams, rows, width), reflectance.dtype),
            pltpu.VMEM((lights * rows, width), reflectance.dtype),
            pltpu.VMEM((2 * rank, lights * rows), jnp.bfloat16),
            pltpu.VMEM((lights * rows, rank), jnp.float32),
            dma((2,)), dma((parts,)), dma((lights,)),
            dma((lights - 1, parts)), dma((lights - 1, parts)),
            dma((lights - 1, blocks)), dma((lights - 1, blocks)),
        ],
        compiler_params=pltpu.CompilerParams(
            collective_id=collective_id, has_side_effects=True, vmem_limit_bytes=40 * 1024 * 1024
        ),
    )(reflectance, pair)


def exchange_kernel(lights, src_ref, dst_ref, bounce, local_sem, send_sem, recv_sem):
    me = lax.axis_index("light")
    peers = [lax.rem(me + step, lights) for step in range(1, lights)]
    greet(pltpu.get_barrier_semaphore(), [{"light": peer} for peer in peers])
    parts, width = src_ref.shape[1], src_ref.shape[3]
    copies = []
    for part in range(parts):
        for slot, peer in enumerate(peers):
            copy = pltpu.make_async_remote_copy(
                src_ref=src_ref.at[peer, part],
                dst_ref=dst_ref.at[me, :, pl.ds(part * width, width)],
                send_sem=send_sem.at[slot, part],
                recv_sem=recv_sem.at[slot, part],
                device_id={"light": peer},
                device_id_type=MESH,
            )
            copy.start()
            copies.append(copy)
    for part in range(parts):
        inward = pltpu.make_async_copy(src_ref.at[me, part], bounce.at[part], local_sem.at[0, part])
        inward.start()
        inward.wait()
        outward = pltpu.make_async_copy(
            bounce.at[part], dst_ref.at[me, :, pl.ds(part * width, width)], local_sem.at[1, part]
        )
        outward.start()
        outward.wait()
    for copy in copies:
        copy.wait()


def exchange(blocks, collective_id):
    lights, parts, rows, width = blocks.shape
    return pl.pallas_call(
        functools.partial(exchange_kernel, lights),
        out_shape=jax.ShapeDtypeStruct((lights, rows, parts * width), blocks.dtype),
        in_specs=[pl.BlockSpec(memory_space=pl.ANY)],
        out_specs=pl.BlockSpec(memory_space=pl.ANY),
        scratch_shapes=[
            pltpu.VMEM(blocks.shape[1:], blocks.dtype),
            pltpu.SemaphoreType.DMA((2, parts)),
            pltpu.SemaphoreType.DMA((lights - 1, parts)),
            pltpu.SemaphoreType.DMA((lights - 1, parts)),
        ],
        compiler_params=pltpu.CompilerParams(
            collective_id=collective_id, has_side_effects=True
        ),
    )(blocks)


def total_kernel(lights, pixes, cams, part_ref, out_ref, plane_buf, light_buf, own_buf,
                 send1, recv1, send2, recv2, send3, recv3):
    light = lax.axis_index("light")
    plane = pixes * cams
    me = lax.axis_index("pix") * cams + lax.axis_index("cam")
    rows = part_ref.shape[0] // plane

    def row_slice(index):
        return pl.ds(pl.multiple_of(index * rows, rows), rows)

    peers = [lax.rem(me + step, plane) for step in range(1, plane)]
    plane_devices = [{"pix": peer // cams, "cam": lax.rem(peer, cams)} for peer in peers]
    light_devices = [{"light": lax.rem(light + step, lights)} for step in range(1, lights)]
    greet(pltpu.get_barrier_semaphore(), plane_devices + light_devices)

    copies = []
    for slot, (peer, device) in enumerate(zip(peers, plane_devices)):
        copy = pltpu.make_async_remote_copy(
            src_ref=part_ref.at[row_slice(peer)],
            dst_ref=plane_buf.at[slot],
            send_sem=send1.at[slot],
            recv_sem=recv1.at[slot],
            device_id=device,
            device_id_type=MESH,
        )
        copy.start()
        copies.append(copy)
    total = part_ref[row_slice(me), :].astype(jnp.float32)
    for slot, copy in enumerate(copies):
        copy.wait_recv()
        total += plane_buf[slot].astype(jnp.float32)
    own_buf[...] = total.astype(own_buf.dtype)

    light_copies = []
    for slot, device in enumerate(light_devices):
        copy = pltpu.make_async_remote_copy(
            src_ref=own_buf,
            dst_ref=light_buf.at[light],
            send_sem=send2.at[slot],
            recv_sem=recv2.at[slot],
            device_id=device,
            device_id_type=MESH,
        )
        copy.start()
        light_copies.append(copy)
    light_buf[light] = own_buf[...]
    for copy in light_copies:
        copy.wait_recv()
    total = light_buf[0].astype(jnp.float32)
    for index in range(1, lights):
        total += light_buf[index].astype(jnp.float32)
    out_ref[row_slice(me), :] = total.astype(out_ref.dtype)

    last_copies = []
    for slot, device in enumerate(plane_devices):
        copy = pltpu.make_async_remote_copy(
            src_ref=out_ref.at[row_slice(me)],
            dst_ref=out_ref.at[row_slice(me)],
            send_sem=send3.at[slot],
            recv_sem=recv3.at[slot],
            device_id=device,
            device_id_type=MESH,
        )
        copy.start()
        last_copies.append(copy)
    for copy in copies + light_copies:
        copy.wait_send()
    for copy in last_copies:
        copy.wait()


def total_over_all(part, collective_id):
    lights, pixes, cams = (lax.axis_size(name) for name in ("light", "pix", "cam"))
    plane = pixes * cams
    rows = part.shape[0] // plane
    block = (rows, part.shape[1])
    dma = pltpu.SemaphoreType.DMA
    return pl.pallas_call(
        functools.partial(total_kernel, lights, pixes, cams),
        out_shape=jax.ShapeDtypeStruct(part.shape, part.dtype),
        in_specs=[pl.BlockSpec(memory_space=pltpu.VMEM)],
        out_specs=pl.BlockSpec(memory_space=pltpu.VMEM),
        scratch_shapes=[
            pltpu.VMEM((plane - 1,) + block, part.dtype),
            pltpu.VMEM((lights,) + block, part.dtype),
            pltpu.VMEM(block, part.dtype),
            dma((plane - 1,)), dma((plane - 1,)),
            dma((lights - 1,)), dma((lights - 1,)),
            dma((plane - 1,)), dma((plane - 1,)),
        ],
        compiler_params=pltpu.CompilerParams(
            collective_id=collective_id, has_side_effects=True
        ),
    )(part)


def orthonormal_kernel(image_ref, basis_ref, pair_ref, whole):
    image = image_ref[...]
    rank = image.shape[1]
    inner = lax.dot_general(image, image, (((0,), (0,)), ((), ())), preferred_element_type=jnp.float32)
    height = 8
    shape = (height, rank)
    sub = lax.broadcasted_iota(jnp.int32, shape, 0)
    lane = lax.broadcasted_iota(jnp.int32, shape, 1)
    count = rank // height
    left = [inner[height * t : height * (t + 1), :] for t in range(count)]
    right = [jnp.where(lane == sub + height * t, 1.0, 0.0) for t in range(count)]

    def spread_row(tile, k):
        return jnp.broadcast_to(tile[k : k + 1, :], shape)

    def spread_column(tile, j):
        return jnp.broadcast_to(tile[:, j : j + 1], shape)

    for p in range(count):
        first = height * p
        top, below = left[p], right[p]
        columns = [spread_column(top, first + k) for k in range(height)]
        inverses, pivots = [], jnp.ones(shape, jnp.float32)
        for k in range(height):
            pivot = spread_row(columns[k], k)
            inverse = 1.0 / pivot
            pivots = jnp.where(sub == k, pivot, pivots)
            inverses.append(inverse)
            factor = jnp.where(sub > k, columns[k] * inverse, 0.0)
            for later in range(k + 1, height):
                columns[later] = columns[later] - factor * spread_row(columns[later], k)
            top = top - factor * spread_row(top, k)
            below = below - factor * spread_row(below, k)
        right[p] = below * lax.rsqrt(pivots)
        top_rows = [spread_row(top, k) * inverses[k] for k in range(height)]
        below_rows = [spread_row(below, k) * inverses[k] for k in range(height)]
        steps = [
            [spread_row(columns[later], k) * inverses[k] for later in range(k + 1, height)]
            for k in range(height)
        ]
        for t in range(p + 1, count):
            own = [spread_column(left[t], first + k) for k in range(height)]
            upper, lower = left[t], right[t]
            for k in range(height):
                for index, later in enumerate(range(k + 1, height)):
                    own[later] = own[later] - own[k] * steps[k][index]
                upper = upper - own[k] * top_rows[k]
                lower = lower - own[k] * below_rows[k]
            left[t], right[t] = upper, lower
    inverse = jnp.concatenate(right, axis=0)
    pieces = []
    for _ in range(3):
        piece = inverse.astype(jnp.bfloat16)
        pieces.append(piece)
        inverse = inverse - piece.astype(jnp.float32)
    basis = None
    for piece in reversed(pieces):
        term = lax.dot_general(
            image, piece, (((1,), (1,)), ((), ())), preferred_element_type=jnp.float32
        )
        basis = term if basis is None else basis + term
    whole[...] = basis
    own = basis_ref.shape[0]
    basis_ref[...] = whole[pl.ds(pl.multiple_of(lax.axis_index("light") * own, own), own), :]
    high = basis.astype(jnp.bfloat16)
    pair_ref[:, :rank] = high
    pair_ref[:, rank:] = (basis - high.astype(jnp.float32)).astype(jnp.bfloat16)


def orthonormal(image):
    rows, rank = image.shape
    own = rows // lax.axis_size("light")
    vmem = pl.BlockSpec(memory_space=pltpu.VMEM)
    return pl.pallas_call(
        orthonormal_kernel,
        out_shape=(
            jax.ShapeDtypeStruct((own, rank), jnp.float32),
            jax.ShapeDtypeStruct((rows, 2 * rank), jnp.bfloat16),
        ),
        in_specs=[vmem],
        out_specs=(vmem, vmem),
        scratch_shapes=[pltpu.VMEM((rows, rank), jnp.float32)],
    )(image)


def per_device(reflectance, start_basis):
    light_rows, camera_cols, pixels = reflectance.shape
    rank_total = start_basis.shape[1]
    light_count = lax.axis_size("light")
    inverse_cols = 1.0 / (camera_cols * pixels * lax.axis_size("cam") * lax.axis_size("pix"))
    own_cols = camera_cols // light_count * pixels
    high = lax.reduce_precision(start_basis, 8, 7)
    pair = jnp.concatenate([high, start_basis - high], axis=1).astype(jnp.bfloat16)
    every_light, image_part = gather_lights(reflectance, pair, inverse_cols, 0)
    every_light = every_light.reshape(light_rows * light_count, own_cols)
    for iteration in range(ITERS):
        if iteration > 0:
            halves = lax.dot_general(
                pair, every_light, (((0,), (0,)), ((), ())), preferred_element_type=jnp.float32
            )
            projected = (halves[:rank_total] + halves[rank_total:]).astype(jnp.bfloat16)
            image_part = lax.dot_general(
                every_light, projected, (((1,), (1,)), ((), ())), preferred_element_type=jnp.float32
            )
            image_part = (image_part * inverse_cols).astype(jnp.bfloat16)
        basis_rows, pair = orthonormal(total_over_all(image_part, 1))
    rank_rows = rank_total // light_count
    core = lax.dot_general(
        pair[:, :rank_total], every_light, (((0,), (0,)), ((), ())),
        preferred_element_type=jnp.float32,
    ).astype(jnp.bfloat16)
    core_rows = exchange(core.reshape(light_count, 1, rank_rows, own_cols), 2)
    core_rows = core_rows.transpose(1, 0, 2).astype(jnp.float32)
    return (core_rows.reshape(rank_rows, camera_cols, pixels), basis_rows)


def solution(mesh):
    placed = (P("light", "cam", "pix"), P())
    return jax.shard_map(
        per_device,
        mesh=mesh,
        in_specs=placed,
        out_specs=(P("light", "cam", "pix"), P("light", None)),
        check_vma=False,
    )
```

```python
import functools

import jax
import jax.numpy as jnp
from jax import lax
from jax.experimental import pallas as pl
from jax.experimental.pallas import tpu as pltpu
from jax.sharding import PartitionSpec as P

ITERS = 2
MESH = pl.DeviceIdType.MESH


def greet(barrier, devices):
    for device in devices:
        pl.semaphore_signal(barrier, inc=1, device_id=device, device_id_type=MESH)
    pl.semaphore_wait(barrier, len(devices))


def gather_kernel(lights, blocks, scale, source_ref, basis_ref, every_ref, image_ref, arrived, turned, tile, left, total,
                  load_sem, own_sem, tile_sem, send_sem, recv_sem, first_send, first_recv):
    me = lax.axis_index("light")
    rows, cams, width = source_ref.shape
    parts = cams // lights
    rank = image_ref.shape[1]
    height = rows // blocks
    step_rows = 16
    peers = [lax.rem(me + step, lights) for step in range(1, lights)]

    def load(block):
        return pltpu.make_async_copy(
            source_ref.at[pl.ds(block * height, height)], arrived.at[block % 2], load_sem.at[block % 2]
        )

    load(0).start()
    greet(pltpu.get_barrier_semaphore(), [{"light": peer} for peer in peers])

    def columns(part):
        return pl.ds(part * width, width)

    def first_copy(slot, peer, block):
        span = pl.ds(block * height, height)
        return pltpu.make_async_remote_copy(
            src_ref=turned.at[peer * parts, span],
            dst_ref=every_ref.at[me, span, columns(0)],
            send_sem=first_send.at[slot, block],
            recv_sem=first_recv.at[slot, block],
            device_id={"light": peer},
            device_id_type=MESH,
        )

    def later_copy(slot, peer, part):
        return pltpu.make_async_remote_copy(
            src_ref=turned.at[peer * parts + part],
            dst_ref=every_ref.at[me, :, columns(part)],
            send_sem=send_sem.at[slot, part],
            recv_sem=recv_sem.at[slot, part],
            device_id={"light": peer},
            device_id_type=MESH,
        )

    copies = [[] for _ in range(parts)]
    for block in range(blocks):
        if block + 1 < blocks:
            load(block + 1).start()
        load(block).wait()

        def turn(index, carry):
            start = pl.multiple_of(index * step_rows, step_rows)
            turned[:, pl.ds(pl.multiple_of(block * height + start, step_rows), step_rows), :] = jnp.transpose(
                arrived[block % 2, pl.ds(start, step_rows)], (1, 0, 2)
            )
            return carry

        lax.fori_loop(0, height // step_rows, turn, 0)
        for slot, peer in enumerate(peers):
            copies[0].append(first_copy(slot, peer, block))
            copies[0][-1].start()
    for part in range(1, parts):
        for slot, peer in enumerate(peers):
            copies[part].append(later_copy(slot, peer, part))
            copies[part][-1].start()
    own = [
        pltpu.make_async_copy(turned.at[me * parts + part], every_ref.at[me, :, columns(part)], own_sem.at[part])
        for part in range(parts)
    ]
    for copy in own:
        copy.start()

    basis = basis_ref[...]
    high = basis.astype(jnp.bfloat16)
    left[:rank] = high.T
    left[rank:] = (basis - high.astype(jnp.float32)).astype(jnp.bfloat16).T
    total[...] = jnp.zeros_like(total)
    chunk = 256
    for part in range(parts):
        own[part].wait()
        for copy in copies[part]:
            copy.wait_recv()
        reads = [
            pltpu.make_async_copy(
                every_ref.at[light, :, columns(part)], tile.at[pl.ds(light * rows, rows)], tile_sem.at[light]
            )
            for light in range(lights)
        ]
        for read in reads:
            read.start()
        for read in reads:
            read.wait()

        def products(index, carry):
            some = tile[:, pl.ds(pl.multiple_of(index * chunk, chunk), chunk)]
            halves = jnp.dot(left[...], some, preferred_element_type=jnp.float32)
            projected = (halves[:rank] + halves[rank:]).astype(jnp.bfloat16)
            total[...] += lax.dot_general(
                some, projected, (((1,), (1,)), ((), ())), preferred_element_type=jnp.float32
            )
            return carry

        lax.fori_loop(0, width // chunk, products, 0)
    image_ref[...] = (total[...] * scale).astype(image_ref.dtype)
    for group in copies:
        for copy in group:
            copy.wait_send()


def gather_lights(reflectance, basis, scale, collective_id):
    rows, cams, width = reflectance.shape
    lights = lax.axis_size("light")
    parts = cams // lights
    blocks = max(1, rows // 64)
    rank = basis.shape[1]
    vmem, anywhere = pl.BlockSpec(memory_space=pltpu.VMEM), pl.BlockSpec(memory_space=pl.ANY)
    dma = pltpu.SemaphoreType.DMA
    return pl.pallas_call(
        functools.partial(gather_kernel, lights, blocks, scale),
        out_shape=(
            jax.ShapeDtypeStruct((lights, rows, parts * width), reflectance.dtype),
            jax.ShapeDtypeStruct((lights * rows, rank), jnp.bfloat16),
        ),
        in_specs=[anywhere, vmem],
        out_specs=(anywhere, vmem),
        scratch_shapes=[
            pltpu.VMEM((2, rows // blocks, cams, width), reflectance.dtype),
            pltpu.VMEM((cams, rows, width), reflectance.dtype),
            pltpu.VMEM((lights * rows, width), reflectance.dtype),
            pltpu.VMEM((2 * rank, lights * rows), jnp.bfloat16),
            pltpu.VMEM((lights * rows, rank), jnp.float32),
            dma((2,)), dma((parts,)), dma((lights,)),
            dma((lights - 1, parts)), dma((lights - 1, parts)),
            dma((lights - 1, blocks)), dma((lights - 1, blocks)),
        ],
        compiler_params=pltpu.CompilerParams(
            collective_id=collective_id, has_side_effects=True, vmem_limit_bytes=40 * 1024 * 1024
        ),
    )(reflectance, basis)


def exchange_kernel(lights, src_ref, dst_ref, bounce, local_sem, send_sem, recv_sem):
    me = lax.axis_index("light")
    peers = [lax.rem(me + step, lights) for step in range(1, lights)]
    greet(pltpu.get_barrier_semaphore(), [{"light": peer} for peer in peers])
    parts, width = src_ref.shape[1], src_ref.shape[3]
    copies = []
    for part in range(parts):
        for slot, peer in enumerate(peers):
            copy = pltpu.make_async_remote_copy(
                src_ref=src_ref.at[peer, part],
                dst_ref=dst_ref.at[me, :, pl.ds(part * width, width)],
                send_sem=send_sem.at[slot, part],
                recv_sem=recv_sem.at[slot, part],
                device_id={"light": peer},
                device_id_type=MESH,
            )
            copy.start()
            copies.append(copy)
    for part in range(parts):
        inward = pltpu.make_async_copy(src_ref.at[me, part], bounce.at[part], local_sem.at[0, part])
        inward.start()
        inward.wait()
        outward = pltpu.make_async_copy(
            bounce.at[part], dst_ref.at[me, :, pl.ds(part * width, width)], local_sem.at[1, part]
        )
        outward.start()
        outward.wait()
    for copy in copies:
        copy.wait()


def exchange(blocks, collective_id):
    lights, parts, rows, width = blocks.shape
    return pl.pallas_call(
        functools.partial(exchange_kernel, lights),
        out_shape=jax.ShapeDtypeStruct((lights, rows, parts * width), blocks.dtype),
        in_specs=[pl.BlockSpec(memory_space=pl.ANY)],
        out_specs=pl.BlockSpec(memory_space=pl.ANY),
        scratch_shapes=[
            pltpu.VMEM(blocks.shape[1:], blocks.dtype),
            pltpu.SemaphoreType.DMA((2, parts)),
            pltpu.SemaphoreType.DMA((lights - 1, parts)),
            pltpu.SemaphoreType.DMA((lights - 1, parts)),
        ],
        compiler_params=pltpu.CompilerParams(
            collective_id=collective_id, has_side_effects=True, vmem_limit_bytes=8 * 1024 * 1024
        ),
    )(blocks)


def total_kernel(lights, pixes, cams, part_ref, out_ref, plane_buf, light_buf, own_buf,
                 send1, recv1, send2, recv2, send3, recv3):
    light = lax.axis_index("light")
    plane = pixes * cams
    me = lax.axis_index("pix") * cams + lax.axis_index("cam")
    rows = part_ref.shape[0] // plane

    def row_slice(index):
        return pl.ds(pl.multiple_of(index * rows, rows), rows)

    peers = [lax.rem(me + step, plane) for step in range(1, plane)]
    plane_devices = [{"pix": peer // cams, "cam": lax.rem(peer, cams)} for peer in peers]
    light_devices = [{"light": lax.rem(light + step, lights)} for step in range(1, lights)]
    greet(pltpu.get_barrier_semaphore(), plane_devices + light_devices)

    copies = []
    for slot, (peer, device) in enumerate(zip(peers, plane_devices)):
        copy = pltpu.make_async_remote_copy(
            src_ref=part_ref.at[row_slice(peer)],
            dst_ref=plane_buf.at[slot],
            send_sem=send1.at[slot],
            recv_sem=recv1.at[slot],
            device_id=device,
            device_id_type=MESH,
        )
        copy.start()
        copies.append(copy)
    total = part_ref[row_slice(me), :].astype(jnp.float32)
    for slot, copy in enumerate(copies):
        copy.wait_recv()
        total += plane_buf[slot].astype(jnp.float32)
    own_buf[...] = total.astype(own_buf.dtype)

    light_copies = []
    for slot, device in enumerate(light_devices):
        copy = pltpu.make_async_remote_copy(
            src_ref=own_buf,
            dst_ref=light_buf.at[light],
            send_sem=send2.at[slot],
            recv_sem=recv2.at[slot],
            device_id=device,
            device_id_type=MESH,
        )
        copy.start()
        light_copies.append(copy)
    light_buf[light] = own_buf[...]
    for copy in light_copies:
        copy.wait_recv()
    total = light_buf[0].astype(jnp.float32)
    for index in range(1, lights):
        total += light_buf[index].astype(jnp.float32)
    out_ref[row_slice(me), :] = total.astype(out_ref.dtype)

    last_copies = []
    for slot, device in enumerate(plane_devices):
        copy = pltpu.make_async_remote_copy(
            src_ref=out_ref.at[row_slice(me)],
            dst_ref=out_ref.at[row_slice(me)],
            send_sem=send3.at[slot],
            recv_sem=recv3.at[slot],
            device_id=device,
            device_id_type=MESH,
        )
        copy.start()
        last_copies.append(copy)
    for copy in copies + light_copies:
        copy.wait_send()
    for copy in last_copies:
        copy.wait()


def total_over_all(part, collective_id):
    lights, pixes, cams = (lax.axis_size(name) for name in ("light", "pix", "cam"))
    plane = pixes * cams
    rows = part.shape[0] // plane
    block = (rows, part.shape[1])
    dma = pltpu.SemaphoreType.DMA
    return pl.pallas_call(
        functools.partial(total_kernel, lights, pixes, cams),
        out_shape=jax.ShapeDtypeStruct(part.shape, part.dtype),
        in_specs=[pl.BlockSpec(memory_space=pltpu.VMEM)],
        out_specs=pl.BlockSpec(memory_space=pltpu.VMEM),
        scratch_shapes=[
            pltpu.VMEM((plane - 1,) + block, part.dtype),
            pltpu.VMEM((lights,) + block, part.dtype),
            pltpu.VMEM(block, part.dtype),
            dma((plane - 1,)), dma((plane - 1,)),
            dma((lights - 1,)), dma((lights - 1,)),
            dma((plane - 1,)), dma((plane - 1,)),
        ],
        compiler_params=pltpu.CompilerParams(
            collective_id=collective_id, has_side_effects=True, vmem_limit_bytes=8 * 1024 * 1024
        ),
    )(part)


def orthonormal_kernel(image_ref, basis_ref, pair_ref, whole):
    image = image_ref[...]
    rank = image.shape[1]
    inner = lax.dot_general(image, image, (((0,), (0,)), ((), ())), preferred_element_type=jnp.float32)
    height = 8
    shape = (height, rank)
    sub = lax.broadcasted_iota(jnp.int32, shape, 0)
    lane = lax.broadcasted_iota(jnp.int32, shape, 1)
    count = rank // height
    left = [inner[height * t : height * (t + 1), :] for t in range(count)]
    right = [jnp.where(lane == sub + height * t, 1.0, 0.0) for t in range(count)]

    def spread_row(tile, k):
        return jnp.broadcast_to(tile[k : k + 1, :], shape)

    def spread_column(tile, j):
        return jnp.broadcast_to(tile[:, j : j + 1], shape)

    for p in range(count):
        first = height * p
        top, below = left[p], right[p]
        columns = [spread_column(top, first + k) for k in range(height)]
        inverses, pivots = [], jnp.ones(shape, jnp.float32)
        for k in range(height):
            pivot = spread_row(columns[k], k)
            inverse = 1.0 / pivot
            pivots = jnp.where(sub == k, pivot, pivots)
            inverses.append(inverse)
            factor = jnp.where(sub > k, columns[k] * inverse, 0.0)
            for later in range(k + 1, height):
                columns[later] = columns[later] - factor * spread_row(columns[later], k)
            top = top - factor * spread_row(top, k)
            below = below - factor * spread_row(below, k)
        right[p] = below * lax.rsqrt(pivots)
        top_rows = [spread_row(top, k) * inverses[k] for k in range(height)]
        below_rows = [spread_row(below, k) * inverses[k] for k in range(height)]
        steps = [
            [spread_row(columns[later], k) * inverses[k] for later in range(k + 1, height)]
            for k in range(height)
        ]
        for t in range(p + 1, count):
            own = [spread_column(left[t], first + k) for k in range(height)]
            upper, lower = left[t], right[t]
            for k in range(height):
                for index, later in enumerate(range(k + 1, height)):
                    own[later] = own[later] - own[k] * steps[k][index]
                upper = upper - own[k] * top_rows[k]
                lower = lower - own[k] * below_rows[k]
            left[t], right[t] = upper, lower
    inverse = jnp.concatenate(right, axis=0)
    pieces = []
    for _ in range(3):
        piece = inverse.astype(jnp.bfloat16)
        pieces.append(piece)
        inverse = inverse - piece.astype(jnp.float32)
    basis = None
    for piece in reversed(pieces):
        term = lax.dot_general(
            image, piece, (((1,), (1,)), ((), ())), preferred_element_type=jnp.float32
        )
        basis = term if basis is None else basis + term
    whole[...] = basis
    own = basis_ref.shape[0]
    basis_ref[...] = whole[pl.ds(pl.multiple_of(lax.axis_index("light") * own, own), own), :]
    high = basis.astype(jnp.bfloat16)
    pair_ref[:, :rank] = high
    pair_ref[:, rank:] = (basis - high.astype(jnp.float32)).astype(jnp.bfloat16)


def orthonormal(image):
    rows, rank = image.shape
    own = rows // lax.axis_size("light")
    vmem = pl.BlockSpec(memory_space=pltpu.VMEM)
    return pl.pallas_call(
        orthonormal_kernel,
        out_shape=(
            jax.ShapeDtypeStruct((own, rank), jnp.float32),
            jax.ShapeDtypeStruct((rows, 2 * rank), jnp.bfloat16),
        ),
        in_specs=[vmem],
        out_specs=(vmem, vmem),
        scratch_shapes=[pltpu.VMEM((rows, rank), jnp.float32)],
        compiler_params=pltpu.CompilerParams(vmem_limit_bytes=16 * 1024 * 1024),
    )(image)


def per_device(reflectance, start_basis):
    light_rows, camera_cols, pixels = reflectance.shape
    rank_total = start_basis.shape[1]
    light_count = lax.axis_size("light")
    inverse_cols = 1.0 / (camera_cols * pixels * lax.axis_size("cam") * lax.axis_size("pix"))
    own_cols = camera_cols // light_count * pixels
    every_light, image_part = gather_lights(reflectance, start_basis, inverse_cols, 0)
    every_light = every_light.reshape(light_rows * light_count, own_cols)
    for iteration in range(ITERS):
        if iteration > 0:
            halves = lax.dot_general(
                pair, every_light, (((0,), (0,)), ((), ())), preferred_element_type=jnp.float32
            )
            projected = (halves[:rank_total] + halves[rank_total:]).astype(jnp.bfloat16)
            image_part = lax.dot_general(
                every_light, projected, (((1,), (1,)), ((), ())), preferred_element_type=jnp.float32
            )
            image_part = (image_part * inverse_cols).astype(jnp.bfloat16)
        basis_rows, pair = orthonormal(total_over_all(image_part, 1))
    rank_rows = rank_total // light_count
    core = lax.dot_general(
        pair[:, :rank_total], every_light, (((0,), (0,)), ((), ())),
        preferred_element_type=jnp.float32,
    ).astype(jnp.bfloat16)
    core_rows = exchange(core.reshape(light_count, 1, rank_rows, own_cols), 2)
    core_rows = core_rows.transpose(1, 0, 2).astype(jnp.float32)
    return (core_rows.reshape(rank_rows, camera_cols, pixels), basis_rows)


def solution(mesh):
    placed = (P("light", "cam", "pix"), P())
    return jax.shard_map(
        per_device,
        mesh=mesh,
        in_specs=placed,
        out_specs=(P("light", "cam", "pix"), P("light", None)),
        check_vma=False,
    )
```
